32 devices in a mesh: dir: 4 (over x, core), chan: 8 (over z, y).
Axes of the slice: x: 2, y: 2, z: 4, core: 2. Of those that a mesh axis runs over, the one named last changes fastest.
Arguments:
- visibilities: float32 [8, 256, 2, 256], P('chan'), may hold values from -4 to 4, as said below
- station_uv: float32 [2, 256], replicated, may hold values from -50 to 50
- source_lm: float32 [2, 64, 32], P(None, 'dir'), may hold values from -0.1 to 0.1
- source_flux: float32 [64, 32], P('dir'), may hold values from 0.01 to 0.1
- band_offset: float32 [8], P('chan'), may hold values from -1 to 1, as said below
- gains_init: float32 [2, 64, 8, 256], P(None, 'dir', 'chan'), may hold values from -1 to 2
- duals_init: float32 [2, 64, 8, 256], P(None, 'dir', 'chan'), may hold values from -3 to 3
- poly_init: float32 [2, 64, 1024], P(None, 'dir'), may hold values from -3 to 3
- penalty: float32 [64], P('dir'), may hold values from 1 to 8
- harmonics: float32 [64, 225], replicated, may hold values from -0.75 to 0.75
- threshold: float32 [1], replicated, may hold values from 0.1 to 0.4
Outputs:
- gains_new: float32 [2, 64, 8, 256], P(None, 'dir', 'chan')
- duals_new: float32 [2, 64, 8, 256], P(None, 'dir', 'chan')
- consensus: float32 [2, 64, 1024], P(None, 'dir')
The draws below stay inside these ranges and needn't reach their ends.
Inputs may be any that keep to these rules, and one draw needn't show every extreme that they name: visibilities[c, p, 0, q] = visibilities[c, q, 0, p] and visibilities[c, p, 1, q] = -visibilities[c, q, 1, p]. `band_offset`: strictly increasing.
All inputs are finite; a program needn't handle non-finite values.
Results may differ from the reference program's by a relative error of at most 0.0003.
Values sent between devices are 32-bit elements; how exact they have to be, the bound alone decides.
A program may use at most 64 MiB of HBM per device.

```python
import math
import jax
import jax.numpy as jnp
from jax import lax

S = 256
NSRC = 32
MODES = 225
NTERM = 4
SWEEPS = 2
K = 64
NCH = 8


def draw_band_offset(key, part):
    position = jnp.arange(NCH).astype(jnp.float32)
    jitter = jax.random.uniform(key, (NCH,), jnp.float32, -0.4, 0.4)
    return -1.0 + (2.0 * position + 1.0 + jitter) / NCH


def draw_gains_init(key, part):
    first_key, second_key = jax.random.split(key)
    dims = (K, NCH, S)
    real_part = 1.0 + 0.25 * jax.random.truncated_normal(first_key, -4.0, 4.0, dims, jnp.float32)
    imag_part = 0.25 * jax.random.truncated_normal(second_key, -4.0, 4.0, dims, jnp.float32)
    return jnp.stack([real_part, imag_part])


def draw_visibilities(key, part):
    first_key, second_key = jax.random.split(key)
    dims = (NCH, S, S)
    sym_draw = jax.random.truncated_normal(first_key, -4.0, 4.0, dims, jnp.float32)
    anti_draw = jax.random.truncated_normal(second_key, -4.0, 4.0, dims, jnp.float32)
    real_part = 0.5 * (sym_draw + jnp.swapaxes(sym_draw, 1, 2))
    imag_part = 0.5 * (anti_draw - jnp.swapaxes(anti_draw, 1, 2))
    return jnp.stack([real_part, imag_part], axis=2)


def level_of(key, extent, shards, smallest, largest):
    level, own = 1.0, jax.random.fold_in(key, 6)
    for dim, parts in shards:
        steps = jnp.exp(jax.random.uniform(jax.random.fold_in(own, dim), (parts,), jnp.float32, smallest / len(shards), largest / len(shards)))
        level = level * jnp.repeat(steps, extent[dim] // parts).reshape([-1 if axis == dim else 1 for axis in range(len(extent))])
    return level


def bell_draw(own_key, shape, deviation, reach, cuts=(), kind=jnp.bfloat16):
    drawn = deviation * jax.random.normal(own_key, shape, jnp.float32)
    if cuts:
        drawn = drawn * level_of(own_key, shape, cuts, -0.22, 0.18)
    return jnp.clip(drawn, -reach, reach).astype(kind)


def setup_inputs(seed: int = 0) -> dict:
    seeds = jax.random.split(jax.random.key(seed), 12)
    visibilities = draw_visibilities(jax.random.fold_in(seeds[11], 71), 0)
    station_uv = jnp.clip(jax.random.uniform(seeds[1], (2, S), jnp.float32, -50.0, 50.0), -50.0, 50.0)
    source_lm = jnp.clip(jax.random.uniform(seeds[2], (2, K, NSRC), jnp.float32, -0.1, 0.1) * level_of(seeds[2], (2, K, NSRC), ((1, 4),), -0.4, 0.0), -0.1, 0.1)
    source_flux = jnp.clip(jnp.exp(math.log(0.1) - 2.3025851 * jax.random.uniform(seeds[3], (K, NSRC), jnp.float32) ** level_of(seeds[3], (K, NSRC), ((0, 4),), -0.2, 0.2)), 0.01, 0.1)
    band_offset = draw_band_offset(jax.random.fold_in(seeds[11], 71), 0)
    gains_init = draw_gains_init(jax.random.fold_in(seeds[11], 71), 0)
    duals_init = bell_draw(seeds[6], (2, K, NCH, S), 0.5, 3.0, ((1, 4), (2, 8)), jnp.float32)
    poly_init = bell_draw(seeds[7], (2, K, S * NTERM), 0.5, 3.0, ((1, 4),), jnp.float32)
    penalty = jnp.clip(jnp.exp(math.log(8.0) - 2.0794415 * jax.random.uniform(seeds[8], (K,), jnp.float32) ** level_of(seeds[8], (K,), ((0, 4),), -0.2, 0.2)), 1.0, 8.0)
    harmonics = bell_draw(seeds[9], (K, MODES), K ** -0.5, 0.75, (), jnp.float32)
    threshold = jnp.clip(jax.random.uniform(seeds[10], (1,), jnp.float32, 0.1, 0.4), 0.1, 0.4)
    return dict(visibilities=visibilities, station_uv=station_uv, source_lm=source_lm, source_flux=source_flux, band_offset=band_offset, gains_init=gains_init, duals_init=duals_init, poly_init=poly_init, penalty=penalty, harmonics=harmonics, threshold=threshold)


highest_degree = lax.Precision.HIGHEST

def legendre(offset):
    return jnp.stack([jnp.ones_like(offset), offset, 0.5 * (3.0 * offset * offset - 1.0), 0.5 * (5.0 * offset * offset * offset - 3.0 * offset)], axis=0)

def gram_inverse(offsets):
    values = legendre(offsets)
    gram = jnp.dot(values, values.T, precision=highest_degree)
    factor = jnp.linalg.cholesky(gram)
    return jax.scipy.linalg.cho_solve((factor, True), jnp.eye(4, dtype=gram.dtype))

def phases(station_uv, source_lm, band_value):
    turns = 2.0 * math.pi * (1.0 + 0.25 * band_value)
    phase_arg = turns * (station_uv[0][:, None, None] * source_lm[0][None] + station_uv[1][:, None, None] * source_lm[1][None])
    return (jnp.cos(phase_arg), jnp.sin(phase_arg))

def refine(res_re, res_im, fringe_real, fringe_imaginary, flux_grp, start_re, start_im, goal_re, goal_im, weight):
    stations, groups, sources = fringe_real.shape
    weighted_real = fringe_real * flux_grp[None]
    weighted_imaginary = fringe_imaginary * flux_grp[None]
    coherency_real = jnp.einsum('ivd,gvd->vig', weighted_real, fringe_real, precision=highest_degree) + jnp.einsum('ivd,gvd->vig', weighted_imaginary, fringe_imaginary, precision=highest_degree)
    coherency_imaginary = jnp.einsum('ivd,gvd->vig', weighted_imaginary, fringe_real, precision=highest_degree) - jnp.einsum('ivd,gvd->vig', weighted_real, fringe_imaginary, precision=highest_degree)
    power_map = coherency_real * coherency_real + coherency_imaginary * coherency_imaginary
    gain_re, gain_im = (start_re, start_im)
    for repeat in range(SWEEPS):
        lift_re = fringe_real * gain_re.T[:, :, None] - fringe_imaginary * gain_im.T[:, :, None]
        lift_im = fringe_real * gain_im.T[:, :, None] + fringe_imaginary * gain_re.T[:, :, None]
        flat_re = lift_re.reshape(stations, groups * sources)
        flat_im = lift_im.reshape(stations, groups * sources)
        hold_re = (jnp.dot(res_re, flat_re, precision=highest_degree) - jnp.dot(res_im, flat_im, precision=highest_degree)).reshape(stations, groups, sources)
        hold_im = (jnp.dot(res_re, flat_im, precision=highest_degree) + jnp.dot(res_im, flat_re, precision=highest_degree)).reshape(stations, groups, sources)
        data_re = lax.optimization_barrier(jnp.sum(weighted_real * hold_re + weighted_imaginary * hold_im, axis=2)).T
        data_im = lax.optimization_barrier(jnp.sum(weighted_real * hold_im - weighted_imaginary * hold_re, axis=2)).T
        mix_re = start_re * gain_re + start_im * gain_im
        mix_im = start_re * gain_im - start_im * gain_re
        totals = jnp.einsum('kpq,ckq->ckp', power_map, jnp.stack([mix_re, mix_im, gain_re * gain_re + gain_im * gain_im]), precision=highest_degree)
        own_re = start_re * totals[0] - start_im * totals[1]
        own_im = start_re * totals[1] + start_im * totals[0]
        denominator = totals[2] + weight[:, None]
        gain_re = (data_re + own_re + weight[:, None] * goal_re) / denominator
        gain_im = (data_im + own_im + weight[:, None] * goal_im) / denominator
    return (gain_re, gain_im)

def shrink(columns, harmonics, cutoff):
    coeffs = jnp.einsum('km,cki->cmi', harmonics, columns, precision=highest_degree)
    magnitude = jnp.sqrt(coeffs[0] * coeffs[0] + coeffs[1] * coeffs[1])
    factor = jnp.maximum(magnitude - cutoff, 0.0) / jnp.maximum(magnitude, cutoff)
    return jnp.einsum('km,cmi->cki', harmonics, coeffs * factor[None], precision=highest_degree)

def reference(visibilities, station_uv, source_lm, source_flux, band_offset, gains_init, duals_init, poly_init, penalty, harmonics, threshold):
    legendre_all = legendre(band_offset)
    inverse = gram_inverse(band_offset)
    poly_shaped = poly_init.reshape(2, K, S, NTERM)

    def one_channel(chan_index):
        band_value = band_offset[chan_index]
        legendre_at = legendre(band_value)
        fringe_real, fringe_imaginary = phases(station_uv, source_lm, band_value)
        start = gains_init[:, :, chan_index, :]
        dual_now = duals_init[:, :, chan_index, :]
        field_re = (fringe_real * start[0].T[:, :, None] - fringe_imaginary * start[1].T[:, :, None]).reshape(S, K * NSRC)
        field_im = (fringe_real * start[1].T[:, :, None] + fringe_imaginary * start[0].T[:, :, None]).reshape(S, K * NSRC)
        flat_flux = source_flux.reshape(-1)
        model_re = jnp.dot(field_re * flat_flux, field_re.T, precision=highest_degree) + jnp.dot(field_im * flat_flux, field_im.T, precision=highest_degree)
        model_im = jnp.dot(field_im * flat_flux, field_re.T, precision=highest_degree) - jnp.dot(field_re * flat_flux, field_im.T, precision=highest_degree)
        res_re = visibilities[chan_index, :, 0, :] - model_re
        res_im = visibilities[chan_index, :, 1, :] - model_im
        target = lax.optimization_barrier(jnp.sum(poly_shaped * legendre_at, axis=3)) - dual_now / penalty[None, :, None]

        def one_cluster(cluster_index):
            gain_re, gain_im = refine(res_re, res_im, lax.dynamic_slice_in_dim(fringe_real, cluster_index, 1, 1), lax.dynamic_slice_in_dim(fringe_imaginary, cluster_index, 1, 1), lax.dynamic_slice_in_dim(source_flux, cluster_index, 1, 0), lax.dynamic_slice_in_dim(start[0], cluster_index, 1, 0), lax.dynamic_slice_in_dim(start[1], cluster_index, 1, 0), lax.dynamic_slice_in_dim(target[0], cluster_index, 1, 0), lax.dynamic_slice_in_dim(target[1], cluster_index, 1, 0), lax.dynamic_slice_in_dim(penalty, cluster_index, 1, 0))
            return jnp.stack([gain_re[0], gain_im[0]])
        solved = lax.map(one_cluster, jnp.arange(K).astype(jnp.int32))
        return jnp.transpose(solved, (1, 0, 2))
    solved_all = lax.map(one_channel, jnp.arange(NCH).astype(jnp.int32))
    gains_new = jnp.transpose(solved_all, (1, 2, 0, 3))
    spread = gains_new + duals_init / penalty[None, :, None, None]
    moments = jnp.einsum('ckfp,tf->ckpt', spread, legendre_all, precision=highest_degree)
    settled = jnp.einsum('ckpt,ut->ckpu', moments, inverse, precision=highest_degree).reshape(2, K, S * NTERM)
    consensus = shrink(settled, harmonics, threshold[0])
    fitted = jnp.einsum('ckpt,tf->ckfp', consensus.reshape(2, K, S, NTERM), legendre_all, precision=highest_degree)
    duals_new = duals_init + penalty[None, :, None, None] * (gains_new - fitted)
    return (gains_new, duals_new, consensus)
```

```python
import functools
import math

import jax
import jax.numpy as jnp
import numpy as np
from jax import lax
from jax.experimental import pallas as pl
from jax.experimental.pallas import tpu as pltpu
from jax.sharding import PartitionSpec as P

NTERM = 4
SWEEPS = 2
MESH = pl.DeviceIdType.MESH
highest = lax.Precision.HIGHEST
VM = pl.BlockSpec(memory_space=pltpu.VMEM)


def fit_circle():
    nodes = np.cos(np.pi * (np.arange(400) + 0.5) / 800.0) * 0.5
    square = nodes * nodes
    scale = 0.25
    sine = np.polynomial.chebyshev.Chebyshev.fit(
        square, np.sin(2 * np.pi * nodes) / nodes, 5, domain=[0, scale], w=nodes
    ).convert(kind=np.polynomial.Polynomial)
    cosine = np.polynomial.chebyshev.Chebyshev.fit(
        square, np.cos(2 * np.pi * nodes), 6, domain=[0, scale]
    ).convert(kind=np.polynomial.Polynomial)
    return [float(c) for c in sine.coef], [float(c) for c in cosine.coef]


SINE, COSINE = fit_circle()


def horner(coefs, x):
    total = coefs[-1] * x + coefs[-2]
    for c in coefs[-3::-1]:
        total = total * x + c
    return total


def circle(turns):
    r = turns - jnp.round(turns)
    square = r * r
    return horner(COSINE, square), r * horner(SINE, square)


def legendre(x):
    return [
        jnp.ones_like(x),
        x,
        0.5 * (3.0 * x * x - 1.0),
        0.5 * (5.0 * x * x * x - 3.0 * x),
    ]


def split(x):
    high = x.astype(jnp.bfloat16)
    low = (x - high.astype(jnp.float32)).astype(jnp.bfloat16)
    return high, low


def tdot(a, b):
    return lax.dot_general(a, b, (((0,), (0,)), ((), ())), preferred_element_type=jnp.float32)


def meet(n_dir, n_chan, me_d, me_c):
    barrier = pltpu.get_barrier_semaphore()
    for j in range(1, n_dir):
        pl.semaphore_signal(
            barrier, inc=1, device_id={"dir": lax.rem(me_d + j, n_dir)}, device_id_type=MESH
        )
    for j in range(1, n_chan):
        pl.semaphore_signal(
            barrier, inc=1, device_id={"chan": lax.rem(me_c + j, n_chan)}, device_id_type=MESH
        )
    pl.semaphore_wait(barrier, n_dir + n_chan - 2)


def gather_kernel(
    n_dir, n_chan, g_ref, s_ref, b_ref, g_all, s_all, b_all, gs, gr, ss, sr, bs, br
):
    me_d, me_c = lax.axis_index("dir"), lax.axis_index("chan")
    meet(n_dir, n_chan, me_d, me_c)
    copies = []
    for j in range(1, n_dir):
        peer = {"dir": lax.rem(me_d + n_dir - j, n_dir)}
        for src, dst, a, b in ((g_ref, g_all, gs, gr), (s_ref, s_all, ss, sr)):
            copies.append(
                pltpu.make_async_remote_copy(
                    src_ref=src,
                    dst_ref=dst.at[j],
                    send_sem=a.at[j],
                    recv_sem=b.at[j],
                    device_id=peer,
                    device_id_type=MESH,
                )
            )
    for j in range(1, n_chan):
        peer = {"chan": lax.rem(me_c + n_chan - j, n_chan)}
        copies.append(
            pltpu.make_async_remote_copy(
                src_ref=b_ref,
                dst_ref=b_all.at[j],
                send_sem=bs.at[j],
                recv_sem=br.at[j],
                device_id=peer,
                device_id_type=MESH,
            )
        )
    for c in copies:
        c.start()
    g_all[0] = g_ref[...]
    s_all[0] = s_ref[...]
    b_all[0] = b_ref[...]
    for c in copies:
        c.wait()


def solve_kernel(
    n_dir,
    n_chan,
    sources,
    b_all,
    uv,
    g_all,
    s_all,
    vis,
    dual,
    poly,
    pen,
    gains,
    zout,
    src_t,
    er,
    ei,
    macc,
    rows,
):
    pair, stations = dual.shape
    clusters = pair // 2
    here = b_all[0, 0:1, 0:1]
    stretch = 1.0 + 0.25 * here
    u = uv[0:1, :] * stretch
    v = uv[1:2, :] * stretch
    chunk = math.gcd(clusters, 4)
    chunks = clusters // chunk
    span = chunk * sources
    macc[...] = jnp.zeros_like(macc)

    def step(d, c, keep):
        start = pl.multiple_of(c * span, span)
        cols = src_t[pl.ds(start, span), :]
        weight = cols[:, 2:3]
        e_r, e_i = circle(cols[:, 0:1] * u + cols[:, 1:2] * v)
        if keep:
            er[pl.ds(start, span), :] = e_r
            ei[pl.ds(start, span), :] = e_i
        f_r, f_i = [], []
        for i in range(chunk):
            a = g_all[d, pl.ds(c * chunk + i, 1), :]
            b = g_all[d, pl.ds(clusters + c * chunk + i, 1), :]
            part_r = e_r[i * sources : (i + 1) * sources]
            part_i = e_i[i * sources : (i + 1) * sources]
            f_r.append(part_r * a - part_i * b)
            f_i.append(part_r * b + part_i * a)
        f_r = jnp.concatenate(f_r, axis=0)
        f_i = jnp.concatenate(f_i, axis=0)
        left = jnp.concatenate([f_r * weight, f_i * weight], axis=0)
        lh, ll = split(left)
        rh, rl = split(f_r)
        ih, il = split(f_i)
        high = jnp.concatenate(
            [jnp.concatenate([rh, ih], axis=0), jnp.concatenate([-ih, rh], axis=0)], axis=1
        )
        low = jnp.concatenate(
            [jnp.concatenate([rl, il], axis=0), jnp.concatenate([-il, rl], axis=0)], axis=1
        )
        macc[...] += tdot(lh, high) + (tdot(lh, low) + tdot(ll, high))

    def others(d, carry):
        src_t[...] = jnp.transpose(s_all[d])
        lax.fori_loop(0, chunks, lambda c, x: (step(d, c, False), x)[1], 0)
        return carry

    lax.fori_loop(1, n_dir, others, 0)
    src_t[...] = jnp.transpose(s_all[0])
    lax.fori_loop(0, chunks, lambda c, x: (step(0, c, True), x)[1], 0)
    macc[:, :stations] = vis[0] - macc[:, :stations]
    macc[:, stations:] = vis[1] - macc[:, stations:]

    level = legendre(here)
    row = lax.broadcasted_iota(jnp.int32, (stations * NTERM, stations), 0)
    col = lax.broadcasted_iota(jnp.int32, (stations * NTERM, stations), 1)
    rest = row - NTERM * col
    pick = jnp.zeros((stations * NTERM, stations), jnp.float32)
    for t in range(NTERM):
        pick = jnp.where(rest == t, level[t], pick)
    pull = jnp.concatenate([pen[...], pen[...]], axis=0)
    offset = dual[...] / pull
    target = jnp.dot(poly[...], pick, precision=highest) - offset
    goal = target * pull
    for k in range(clusters):
        rows[k, 0:1, :] = g_all[0, k : k + 1, :]
        rows[k, 1:2, :] = g_all[0, clusters + k : clusters + k + 1, :]
        rows[k, 2:3, :] = goal[k : k + 1]
        rows[k, 3:4, :] = goal[clusters + k : clusters + k + 1]
        rows[k, 4:5, :] = jnp.broadcast_to(pen[k : k + 1, :], (1, stations))
        rows[k, 5:8, :] = jnp.zeros((3, stations), jnp.float32)

    def solve(k, carry):
        start = pl.multiple_of(k * sources, sources)
        e_r = er[pl.ds(start, sources), :]
        e_i = ei[pl.ds(start, sources), :]
        weight = src_t[pl.ds(start, sources), :][:, 2:3]
        lh, ll = split(jnp.concatenate([e_r * weight, e_i * weight], axis=0))
        rh, rl = split(
            jnp.concatenate(
                [jnp.concatenate([e_r, e_i], axis=0), jnp.concatenate([-e_i, e_r], axis=0)],
                axis=1,
            )
        )
        coherency = tdot(
            jnp.concatenate([lh, lh, ll], axis=0), jnp.concatenate([rh, rl, rh], axis=0)
        )
        c_r = coherency[:, :stations]
        c_i = coherency[:, stations:]
        r_r = macc[:, :stations]
        r_i = macc[:, stations:]
        power = c_r * c_r + c_i * c_i
        b_r = r_r * c_r + r_i * c_i
        b_i = r_i * c_r - r_r * c_i
        block = rows[k]
        g_r, g_i = block[0:1], block[1:2]
        cols = jnp.transpose(block)
        k_r, k_i = cols[:, 0:1], cols[:, 1:2]
        rho = cols[:, 4:5]
        n_r = jnp.sum(b_r * g_r - b_i * g_i, axis=1, keepdims=True)
        n_i = jnp.sum(b_r * g_i + b_i * g_r, axis=1, keepdims=True)
        total = jnp.sum(power * (g_r * g_r + g_i * g_i), axis=1, keepdims=True)
        inverse = 1.0 / (total + rho)
        h_r = (n_r + k_r * total + cols[:, 2:3]) * inverse
        h_i = (n_i + k_i * total + cols[:, 3:4]) * inverse
        mix_r = k_r * h_r + k_i * h_i
        mix_i = k_r * h_i - k_i * h_r
        m_r = jnp.sum(b_r * h_r + b_i * h_i, axis=0, keepdims=True)
        m_i = jnp.sum(b_r * h_i - b_i * h_r, axis=0, keepdims=True)
        t_0 = jnp.sum(power * mix_r, axis=0, keepdims=True)
        t_1 = jnp.sum(power * mix_i, axis=0, keepdims=True)
        t_2 = jnp.sum(power * (h_r * h_r + h_i * h_i), axis=0, keepdims=True)
        inverse = 1.0 / (t_2 + block[4:5])
        gains[pl.ds(k, 1), :] = (m_r + g_r * t_0 - g_i * t_1 + block[2:3]) * inverse
        gains[pl.ds(clusters + k, 1), :] = (m_i + g_r * t_1 + g_i * t_0 + block[3:4]) * inverse
        return carry

    lax.fori_loop(0, clusters, solve, 0)

    values = legendre(b_all[:, 0, :])
    gram = [
        [jnp.sum(values[t] * values[s], axis=0, keepdims=True) for s in range(t + 1)]
        for t in range(NTERM)
    ]
    factor = [[None] * NTERM for _ in range(NTERM)]
    for t in range(NTERM):
        for s in range(t + 1):
            rest_sum = gram[t][s]
            for r in range(s):
                rest_sum = rest_sum - factor[t][r] * factor[s][r]
            factor[t][s] = jnp.sqrt(rest_sum) if s == t else rest_sum / factor[s][s]
    mine = legendre(b_all[0, 0:1, :])
    half = []
    for t in range(NTERM):
        rest_sum = mine[t]
        for s in range(t):
            rest_sum = rest_sum - factor[t][s] * half[s]
        half.append(rest_sum / factor[t][t])
    taps = [None] * NTERM
    for t in reversed(range(NTERM)):
        rest_sum = half[t]
        for s in range(t + 1, NTERM):
            rest_sum = rest_sum - factor[s][t] * taps[s]
        taps[t] = rest_sum / factor[t][t]
    row = lax.broadcasted_iota(jnp.int32, (stations, stations * NTERM), 0)
    col = lax.broadcasted_iota(jnp.int32, (stations, stations * NTERM), 1)
    rest = col - NTERM * row
    spread_out = jnp.zeros((stations, stations * NTERM), jnp.float32)
    for t in range(NTERM):
        spread_out = jnp.where(rest == t, taps[t][:, 0:1], spread_out)
    z = jnp.dot(gains[...] + offset, spread_out, precision=highest)
    width = stations * NTERM // n_chan
    for j in range(n_chan):
        if width < zout.shape[2]:
            zout[j] = jnp.zeros(zout.shape[1:], jnp.float32)
        zout[j, :, :width] = z[:, j * width : (j + 1) * width]


def smooth_kernel(
    n_dir, n_chan, z_ref, harm, cut, out, zin, own, zall, part, s1, r1, s2, r2, s3, r3
):
    me_d, me_c = lax.axis_index("dir"), lax.axis_index("chan")
    meet(n_dir, n_chan, me_d, me_c)
    pair = own.shape[0]
    clusters = pair // 2

    def send(src, dst, a, b, peer):
        return pltpu.make_async_remote_copy(
            src_ref=src, dst_ref=dst, send_sem=a, recv_sem=b, device_id=peer, device_id_type=MESH
        )

    first = []
    for j in range(1, n_chan):
        peer = lax.rem(me_c + j, n_chan)
        first.append(send(z_ref.at[peer], zin.at[j], s1.at[j], r1.at[j], {"chan": peer}))
    for c in first:
        c.start()
    total = z_ref[me_c]
    for j, c in enumerate(first):
        c.wait_recv()
        total = total + zin[j + 1]
    own[...] = total
    second = []
    for j in range(1, n_dir):
        peer = lax.rem(me_d + j, n_dir)
        second.append(send(own, zall.at[me_d], s2.at[j], r2.at[j], {"dir": peer}))
    for c in second:
        c.start()
    zall[me_d] = total
    for c in second:
        c.wait()
    coeff_r = jnp.concatenate([zall[d][:clusters] for d in range(n_dir)], axis=0)
    coeff_i = jnp.concatenate([zall[d][clusters:] for d in range(n_dir)], axis=0)
    both = jnp.concatenate([coeff_r, coeff_i], axis=1)
    lanes = own.shape[1]
    a = lax.dot_general(
        harm[...],
        both,
        (((0,), (0,)), ((), ())),
        precision=highest,
        preferred_element_type=jnp.float32,
    )
    a_r, a_i = a[:, :lanes], a[:, lanes:]
    size = jnp.sqrt(a_r * a_r + a_i * a_i)
    limit = cut[0:1, 0:1]
    scale = jnp.maximum(size - limit, 0.0) / jnp.maximum(size, limit)
    mine = harm[pl.ds(pl.multiple_of(me_d * clusters, clusters), clusters), :]
    done = jnp.dot(
        mine, jnp.concatenate([a_r * scale, a_i * scale], axis=1), precision=highest
    )
    part[:clusters] = done[:, :lanes]
    part[clusters:] = done[:, lanes:]
    third = []
    for j in range(1, n_chan):
        peer = lax.rem(me_c + j, n_chan)
        third.append(send(part, out.at[me_c], s3.at[j], r3.at[j], {"chan": peer}))
    for c in third:
        c.start()
    out[me_c] = part[...]
    for c in third:
        c.wait()
    for c in first:
        c.wait_send()


def finish_kernel(n_chan, blocks, band, gains, dual, pen, cons_out, dual_out):
    pair, stations = gains.shape
    width = stations * NTERM // n_chan
    level = legendre(band[0:1, 0:1])
    for j in range(n_chan):
        cons_out[:, j * width : (j + 1) * width] = blocks[j][:, :width]
    row = lax.broadcasted_iota(jnp.int32, (stations * NTERM, stations), 0)
    col = lax.broadcasted_iota(jnp.int32, (stations * NTERM, stations), 1)
    rest = row - NTERM * col
    pick = jnp.zeros((stations * NTERM, stations), jnp.float32)
    for t in range(NTERM):
        pick = jnp.where(rest == t, level[t], pick)
    fitted = jnp.dot(cons_out[...], pick, precision=highest)
    pull = jnp.concatenate([pen[...], pen[...]], axis=0)
    dual_out[...] = dual[...] + pull * (gains[...] - fitted)


def solution(mesh):
    n_dir, n_chan = mesh.shape["dir"], mesh.shape["chan"]

    def shards(
        visibilities,
        station_uv,
        source_lm,
        source_flux,
        band_offset,
        gains_init,
        duals_init,
        poly_init,
        penalty,
        harmonics,
        threshold,
    ):
        f32 = jnp.float32
        _, clusters, sources = source_lm.shape
        stations = station_uv.shape[1]
        pair = 2 * clusters
        lanes = max(128, stations * NTERM // n_chan)
        g0 = gains_init.reshape(pair, stations)
        dual = duals_init.reshape(pair, stations)
        poly = poly_init.reshape(pair, stations * NTERM)
        flat = clusters * sources
        table = jnp.concatenate(
            [
                source_lm.reshape(2, flat),
                source_flux.reshape(1, flat),
                jnp.zeros((5, flat), f32),
            ],
            axis=0,
        )
        band = jnp.broadcast_to(band_offset.reshape(1, 1), (8, 128))
        cut = jnp.broadcast_to(threshold.reshape(1, 1), (8, 128))
        pen = penalty.reshape(clusters, 1)
        vis = jnp.transpose(visibilities[0], (1, 0, 2))
        dma = pltpu.SemaphoreType.DMA
        g_all, s_all, b_all = pl.pallas_call(
            functools.partial(gather_kernel, n_dir, n_chan),
            out_shape=(
                jax.ShapeDtypeStruct((n_dir, pair, stations), f32),
                jax.ShapeDtypeStruct((n_dir, 8, flat), f32),
                jax.ShapeDtypeStruct((n_chan, 8, 128), f32),
            ),
            in_specs=[VM] * 3,
            out_specs=(VM,) * 3,
            scratch_shapes=[
                dma((n_dir,)),
                dma((n_dir,)),
                dma((n_dir,)),
                dma((n_dir,)),
                dma((n_chan,)),
                dma((n_chan,)),
            ],
            compiler_params=pltpu.CompilerParams(collective_id=0, has_side_effects=True),
            name="gather_inputs",
        )(g0, table, band)
        gains, z = pl.pallas_call(
            functools.partial(solve_kernel, n_dir, n_chan, sources),
            out_shape=(
                jax.ShapeDtypeStruct((pair, stations), f32),
                jax.ShapeDtypeStruct((n_chan, pair, lanes), f32),
            ),
            in_specs=[VM] * 8,
            out_specs=(VM,) * 2,
            scratch_shapes=[
                pltpu.VMEM((flat, 8), f32),
                pltpu.VMEM((flat, stations), f32),
                pltpu.VMEM((flat, stations), f32),
                pltpu.VMEM((stations, 2 * stations), f32),
                pltpu.VMEM((clusters, 8, stations), f32),
            ],
            name="solve_gains",
        )(b_all, station_uv, g_all, s_all, vis, dual, poly, pen)
        blocks = pl.pallas_call(
            functools.partial(smooth_kernel, n_dir, n_chan),
            out_shape=jax.ShapeDtypeStruct((n_chan, pair, lanes), f32),
            in_specs=[VM] * 3,
            out_specs=VM,
            scratch_shapes=[
                pltpu.VMEM((n_chan, pair, lanes), f32),
                pltpu.VMEM((pair, lanes), f32),
                pltpu.VMEM((n_dir, pair, lanes), f32),
                pltpu.VMEM((pair, lanes), f32),
                dma((n_chan,)),
                dma((n_chan,)),
                dma((n_dir,)),
                dma((n_dir,)),
                dma((n_chan,)),
                dma((n_chan,)),
            ],
            compiler_params=pltpu.CompilerParams(collective_id=1, has_side_effects=True),
            name="smooth",
        )(z, harmonics, cut)
        consensus, duals = pl.pallas_call(
            functools.partial(finish_kernel, n_chan),
            out_shape=(
                jax.ShapeDtypeStruct((pair, stations * NTERM), f32),
                jax.ShapeDtypeStruct((pair, stations), f32),
            ),
            in_specs=[VM] * 5,
            out_specs=(VM,) * 2,
            name="finish",
        )(blocks, band, gains, dual, pen)
        shape = (2, clusters, 1, stations)
        return (
            gains.reshape(shape),
            duals.reshape(shape),
            consensus.reshape(2, clusters, stations * NTERM),
        )

    return jax.shard_map(
        shards,
        mesh=mesh,
        in_specs=(
            P("chan", None, None, None),
            P(),
            P(None, "dir", None),
            P("dir", None),
            P("chan"),
            P(None, "dir", "chan", None),
            P(None, "dir", "chan", None),
            P(None, "dir", None),
            P("dir"),
            P(),
            P(),
        ),
        out_specs=(
            P(None, "dir", "chan", None),
            P(None, "dir", "chan", None),
            P(None, "dir", None),
        ),
        check_vma=False,
    )
```

```python
import functools
import math

import jax
import jax.numpy as jnp
import numpy as np
from jax import lax
from jax.experimental import pallas as pl
from jax.experimental.pallas import tpu as pltpu
from jax.sharding import PartitionSpec as P

NTERM = 4
SWEEPS = 2
MESH = pl.DeviceIdType.MESH
highest = lax.Precision.HIGHEST
VM = pl.BlockSpec(memory_space=pltpu.VMEM)


def fit_circle():
    nodes = np.cos(np.pi * (np.arange(400) + 0.5) / 800.0) * 0.5
    square = nodes * nodes
    scale = 0.25
    sine = np.polynomial.chebyshev.Chebyshev.fit(
        square, np.sin(2 * np.pi * nodes) / nodes, 5, domain=[0, scale], w=nodes
    ).convert(kind=np.polynomial.Polynomial)
    cosine = np.polynomial.chebyshev.Chebyshev.fit(
        square, np.cos(2 * np.pi * nodes), 6, domain=[0, scale]
    ).convert(kind=np.polynomial.Polynomial)
    return [float(c) for c in sine.coef], [float(c) for c in cosine.coef]


SINE, COSINE = fit_circle()


def horner(coefs, x):
    total = coefs[-1] * x + coefs[-2]
    for c in coefs[-3::-1]:
        total = total * x + c
    return total


def circle(turns):
    r = turns - jnp.round(turns)
    square = r * r
    return horner(COSINE, square), r * horner(SINE, square)


def legendre(x):
    return [
        jnp.ones_like(x),
        x,
        0.5 * (3.0 * x * x - 1.0),
        0.5 * (5.0 * x * x * x - 3.0 * x),
    ]


def split(x):
    high = x.astype(jnp.bfloat16)
    low = (x - high.astype(jnp.float32)).astype(jnp.bfloat16)
    return high, low


def tdot(a, b):
    return lax.dot_general(a, b, (((0,), (0,)), ((), ())), preferred_element_type=jnp.float32)


def meet(n_dir, n_chan, me_d, me_c):
    barrier = pltpu.get_barrier_semaphore()
    for j in range(1, n_dir):
        pl.semaphore_signal(
            barrier, inc=1, device_id={"dir": lax.rem(me_d + j, n_dir)}, device_id_type=MESH
        )
    for j in range(1, n_chan):
        pl.semaphore_signal(
            barrier, inc=1, device_id={"chan": lax.rem(me_c + j, n_chan)}, device_id_type=MESH
        )
    pl.semaphore_wait(barrier, n_dir + n_chan - 2)


def column(pen):
    count = pen.shape[1]
    row = lax.broadcasted_iota(jnp.int32, (count, count), 0)
    col = lax.broadcasted_iota(jnp.int32, (count, count), 1)
    return jnp.sum(jnp.where(row == col, pen[...], 0.0), axis=1, keepdims=True)


def step_kernel(
    n_dir,
    n_chan,
    sources,
    vis,
    uv,
    table,
    band,
    g_ref,
    dual_ref,
    poly,
    pen_ref,
    harm,
    cut,
    gains_out,
    dual_out,
    cons_out,
    b_ref,
    g_all,
    s_all,
    b_all,
    src_t,
    er,
    ei,
    macc,
    rows,
    dual,
    gains,
    packed,
    zin,
    own,
    zall,
    part,
    blocks,
    gs,
    gr,
    ss,
    sr,
    bs,
    br,
    s1,
    r1,
    s2,
    r2,
    s3,
    r3,
):
    pair, stations = dual.shape
    clusters = pair // 2
    me_d, me_c = lax.axis_index("dir"), lax.axis_index("chan")
    b_ref[...] = jnp.full(b_ref.shape, band[0], jnp.float32)

    def send(src, dst, a, b, peer):
        return pltpu.make_async_remote_copy(
            src_ref=src, dst_ref=dst, send_sem=a, recv_sem=b, device_id=peer, device_id_type=MESH
        )

    meet(n_dir, n_chan, me_d, me_c)
    copies = []
    for j in range(1, n_dir):
        peer = {"dir": lax.rem(me_d + n_dir - j, n_dir)}
        copies.append(send(g_ref, g_all.at[j], gs.at[j], gr.at[j], peer))
        copies.append(send(table, s_all.at[j], ss.at[j], sr.at[j], peer))
    for j in range(1, n_chan):
        peer = {"chan": lax.rem(me_c + n_chan - j, n_chan)}
        copies.append(send(b_ref, b_all.at[j], bs.at[j], br.at[j], peer))
    for c in copies:
        c.start()
    b_all[0] = b_ref[...]
    g_all[0] = g_ref[...]

    here = b_ref[0:1, 0:1]
    stretch = 1.0 + 0.25 * here
    u = uv[0:1, :] * stretch
    v = uv[1:2, :] * stretch
    chunk = math.gcd(clusters, 4)
    chunks = clusters // chunk
    span = chunk * sources
    macc[:, :stations] = jnp.zeros((stations, stations), jnp.float32)

    def step(d, c, keep):
        start = pl.multiple_of(c * span, span)
        cols = src_t[pl.ds(start, span), :]
        weight = cols[:, 2:3]
        e_r, e_i = circle(cols[:, 0:1] * u + cols[:, 1:2] * v)
        if keep:
            er[pl.ds(start, span), :] = e_r
            ei[pl.ds(start, span), :] = e_i
        f_r, f_i = [], []
        for i in range(chunk):
            a = g_all[d, 0, c * chunk + i]
            b = g_all[d, 1, c * chunk + i]
            part_r = e_r[i * sources : (i + 1) * sources]
            part_i = e_i[i * sources : (i + 1) * sources]
            f_r.append(part_r * a - part_i * b)
            f_i.append(part_r * b + part_i * a)
        f_r = jnp.concatenate(f_r, axis=0)
        f_i = jnp.concatenate(f_i, axis=0)
        lh, ll = split(jnp.concatenate([f_r * weight, f_i * weight], axis=0))
        high, low = split(jnp.concatenate([f_r - f_i, f_i + f_r], axis=0))
        macc[:, :stations] += tdot(lh, high) + (tdot(lh, low) + tdot(ll, high))

    src_t[...] = jnp.transpose(table[...])
    lax.fori_loop(0, chunks, lambda c, x: (step(0, c, True), x)[1], 0)

    for k in range(clusters):
        dual[k : k + 1, :] = dual_ref[0, k]
        dual[clusters + k : clusters + k + 1, :] = dual_ref[1, k]
    level = legendre(here)
    pen = column(pen_ref)
    pull = jnp.concatenate([pen, pen], axis=0)
    tile = 32 * NTERM
    tiles = stations // 32
    row = lax.broadcasted_iota(jnp.int32, (tile, tile), 0)
    col = lax.broadcasted_iota(jnp.int32, (tile, tile), 1)
    pick = jnp.zeros((tile, tile), jnp.float32)
    for t in range(NTERM):
        pick = jnp.where(row - NTERM * col == t, level[t], pick)
    stacked = jnp.concatenate([poly[:, j * tile : (j + 1) * tile] for j in range(tiles)], axis=0)
    value = jnp.dot(stacked, pick, precision=highest)
    value = jnp.concatenate(
        [value[j * pair : (j + 1) * pair, :32] for j in range(tiles)], axis=1
    )
    offset = dual[...] / pull
    goal = (value - offset) * pull
    for k in range(clusters):
        rows[k, 0:1, :] = g_ref[0, k]
        rows[k, 1:2, :] = g_ref[1, k]
        rows[k, 2:3, :] = goal[k : k + 1]
        rows[k, 3:4, :] = goal[clusters + k : clusters + k + 1]
        rows[k, 4:5, :] = jnp.broadcast_to(pen[k : k + 1, :], (1, stations))
        rows[k, 5:8, :] = jnp.zeros((3, stations), jnp.float32)

    for c in copies:
        c.wait()

    def others(d, carry):
        src_t[...] = jnp.transpose(s_all[d])
        lax.fori_loop(0, chunks, lambda c, x: (step(d, c, False), x)[1], 0)
        return carry

    lax.fori_loop(1, n_dir, others, 0)
    src_t[...] = jnp.transpose(table[...])
    both = macc[:, :stations]
    turned = jnp.transpose(both)
    macc[:, :stations] = vis[:, 0, :] - 0.5 * (both + turned)
    macc[:, stations:] = vis[:, 1, :] - 0.5 * (both - turned)

    def solve(k, carry):
        start = pl.multiple_of(k * sources, sources)
        e_r = er[pl.ds(start, sources), :]
        e_i = ei[pl.ds(start, sources), :]
        weight = src_t[pl.ds(start, sources), :][:, 2:3]
        lh, ll = split(jnp.concatenate([e_r * weight, e_i * weight], axis=0))
        rh, rl = split(
            jnp.concatenate(
                [jnp.concatenate([e_r, e_i], axis=0), jnp.concatenate([-e_i, e_r], axis=0)],
                axis=1,
            )
        )
        coherency = tdot(
            jnp.concatenate([lh, lh, ll], axis=0), jnp.concatenate([rh, rl, rh], axis=0)
        )
        c_r = coherency[:, :stations]
        c_i = coherency[:, stations:]
        r_r = macc[:, :stations]
        r_i = macc[:, stations:]
        power = c_r * c_r + c_i * c_i
        b_r = r_r * c_r + r_i * c_i
        b_i = r_i * c_r - r_r * c_i
        block = rows[k]
        g_r, g_i = block[0:1], block[1:2]
        cols = jnp.transpose(block)
        k_r, k_i = cols[:, 0:1], cols[:, 1:2]
        rho = cols[:, 4:5]
        n_r = jnp.sum(b_r * g_r - b_i * g_i, axis=1, keepdims=True)
        n_i = jnp.sum(b_r * g_i + b_i * g_r, axis=1, keepdims=True)
        total = jnp.sum(power * (g_r * g_r + g_i * g_i), axis=1, keepdims=True)
        inverse = 1.0 / (total + rho)
        h_r = (n_r + k_r * total + cols[:, 2:3]) * inverse
        h_i = (n_i + k_i * total + cols[:, 3:4]) * inverse
        mix_r = k_r * h_r + k_i * h_i
        mix_i = k_r * h_i - k_i * h_r
        m_r = jnp.sum(b_r * h_r + b_i * h_i, axis=0, keepdims=True)
        m_i = jnp.sum(b_r * h_i - b_i * h_r, axis=0, keepdims=True)
        t_0 = jnp.sum(power * mix_r, axis=0, keepdims=True)
        t_1 = jnp.sum(power * mix_i, axis=0, keepdims=True)
        t_2 = jnp.sum(power * (h_r * h_r + h_i * h_i), axis=0, keepdims=True)
        inverse = 1.0 / (t_2 + block[4:5])
        new_r = (m_r + g_r * t_0 - g_i * t_1 + block[2:3]) * inverse
        new_i = (m_i + g_r * t_1 + g_i * t_0 + block[3:4]) * inverse
        gains[pl.ds(k, 1), :] = new_r
        gains[pl.ds(clusters + k, 1), :] = new_i
        gains_out[0, k] = new_r
        gains_out[1, k] = new_i
        return carry

    lax.fori_loop(0, clusters, solve, 0)

    spread = gains[...] + offset
    each = stations // n_chan
    groups = pair // 8
    used = groups * each
    lanes = packed.shape[2]
    for j in range(n_chan):
        if used < lanes:
            packed[j] = jnp.zeros((8, lanes), jnp.float32)
        packed[j, :, :used] = jnp.concatenate(
            [spread[8 * g : 8 * g + 8, j * each : (j + 1) * each] for g in range(groups)], axis=1
        )

    first = []
    for j in range(1, n_chan):
        peer = lax.rem(me_c + n_chan - j, n_chan)
        first.append(send(packed.at[peer], zin.at[j], s1.at[j], r1.at[j], {"chan": peer}))
    for c in first:
        c.start()

    everywhere = b_all[:, 0, :]
    values = legendre(everywhere)
    gram = [
        [jnp.sum(values[t] * values[s], axis=0, keepdims=True) for s in range(t + 1)]
        for t in range(NTERM)
    ]
    factor = [[None] * NTERM for _ in range(NTERM)]
    for t in range(NTERM):
        for s in range(t + 1):
            rest_sum = gram[t][s]
            for r in range(s):
                rest_sum = rest_sum - factor[t][r] * factor[s][r]
            factor[t][s] = jnp.sqrt(rest_sum) if s == t else rest_sum / factor[s][s]
    half = []
    for t in range(NTERM):
        rest_sum = values[t]
        for s in range(t):
            rest_sum = rest_sum - factor[t][s] * half[s]
        half.append(rest_sum / factor[t][t])
    taps = [None] * NTERM
    for t in reversed(range(NTERM)):
        rest_sum = half[t]
        for s in range(t + 1, NTERM):
            rest_sum = rest_sum - factor[s][t] * taps[s]
        taps[t] = rest_sum / factor[t][t]

    mixed = [packed[me_c] * taps[t][0:1, 0:1] for t in range(NTERM)]
    for j in range(1, n_chan):
        first[j - 1].wait_recv()
        got = zin[j]
        for t in range(NTERM):
            mixed[t] = mixed[t] + got * taps[t][j : j + 1, 0:1]
    wide = NTERM * each
    if wide < own.shape[1]:
        own[...] = jnp.zeros_like(own)
    for g in range(groups):
        own[8 * g : 8 * g + 8, :wide] = jnp.concatenate(
            [mixed[t][:, g * each : (g + 1) * each] for t in range(NTERM)], axis=1
        )
    second = []
    for j in range(1, n_dir):
        peer = lax.rem(me_d + j, n_dir)
        second.append(send(own, zall.at[me_d], s2.at[j], r2.at[j], {"dir": peer}))
    for c in second:
        c.start()
    zall[me_d] = own[...]
    for c in second:
        c.wait()
    width = own.shape[1]
    coeff_r = jnp.concatenate([zall[d][:clusters] for d in range(n_dir)], axis=0)
    coeff_i = jnp.concatenate([zall[d][clusters:] for d in range(n_dir)], axis=0)
    a = lax.dot_general(
        harm[...],
        jnp.concatenate([coeff_r, coeff_i], axis=1),
        (((0,), (0,)), ((), ())),
        precision=highest,
        preferred_element_type=jnp.float32,
    )
    a_r, a_i = a[:, :width], a[:, width:]
    size = jnp.sqrt(a_r * a_r + a_i * a_i)
    limit = cut[0]
    scale = jnp.maximum(size - limit, 0.0) / jnp.maximum(size, limit)
    mine = harm[pl.ds(pl.multiple_of(me_d * clusters, clusters), clusters), :]
    done = jnp.dot(
        mine, jnp.concatenate([a_r * scale, a_i * scale], axis=1), precision=highest
    )
    part[:clusters] = done[:, :width]
    part[clusters:] = done[:, width:]
    third = []
    for j in range(1, n_chan):
        peer = lax.rem(me_c + j, n_chan)
        third.append(send(part, blocks.at[me_c], s3.at[j], r3.at[j], {"chan": peer}))
    for c in third:
        c.start()
    blocks[me_c] = part[...]
    row = lax.broadcasted_iota(jnp.int32, (width, width), 0)
    col = lax.broadcasted_iota(jnp.int32, (width, width), 1)
    weave = jnp.zeros((width, width), jnp.float32)
    sample = jnp.zeros((width, width), jnp.float32)
    for t in range(NTERM):
        place = row - t * each
        inside = (place >= 0) & (place < each)
        weave = jnp.where(inside & (col == NTERM * place + t), 1.0, weave)
        sample = jnp.where(inside & (col == place), level[t], sample)
    for c in first:
        c.wait_send()
    for c in third:
        c.wait()
    result = jnp.dot(
        jnp.concatenate([blocks[j] for j in range(n_chan)], axis=0),
        jnp.concatenate([weave, sample], axis=1),
        precision=highest,
    )
    fitted = []
    for j in range(n_chan):
        piece = result[j * pair : (j + 1) * pair]
        cons_out[:, j * wide : (j + 1) * wide] = piece[:, :wide]
        fitted.append(piece[:, width : width + each])
    fitted = jnp.concatenate(fitted, axis=1)
    fresh = dual[...] + pull * (gains[...] - fitted)
    for k in range(clusters):
        dual_out[0, k] = fresh[k : k + 1]
        dual_out[1, k] = fresh[clusters + k : clusters + k + 1]


def solution(mesh):
    n_dir, n_chan = mesh.shape["dir"], mesh.shape["chan"]

    def shards(
        visibilities,
        station_uv,
        source_lm,
        source_flux,
        band_offset,
        gains_init,
        duals_init,
        poly_init,
        penalty,
        harmonics,
        threshold,
    ):
        f32 = jnp.float32
        _, clusters, sources = source_lm.shape
        stations = station_uv.shape[1]
        pair = 2 * clusters
        lanes = max(128, stations * NTERM // n_chan)
        poly = poly_init.reshape(pair, stations * NTERM)
        flat = clusters * sources
        table = jnp.concatenate(
            [
                source_lm.reshape(2, flat),
                source_flux.reshape(1, flat),
                jnp.zeros((5, flat), f32),
            ],
            axis=0,
        )
        dma = pltpu.SemaphoreType.DMA
        shape = (2, clusters, 1, stations)
        small = max(128, stations // n_chan * (pair // 8))
        SM = pl.BlockSpec(memory_space=pltpu.SMEM)
        gains, duals, consensus = pl.pallas_call(
            functools.partial(step_kernel, n_dir, n_chan, sources),
            out_shape=(
                jax.ShapeDtypeStruct(shape, f32),
                jax.ShapeDtypeStruct(shape, f32),
                jax.ShapeDtypeStruct((pair, stations * NTERM), f32),
            ),
            in_specs=[VM, VM, VM, SM, VM, VM, VM, VM, VM, SM],
            out_specs=(VM,) * 3,
            scratch_shapes=[
                pltpu.VMEM((8, 128), f32),
                pltpu.VMEM((n_dir,) + shape, f32),
                pltpu.VMEM((n_dir, 8, flat), f32),
                pltpu.VMEM((n_chan, 8, 128), f32),
                pltpu.VMEM((flat, 8), f32),
                pltpu.VMEM((flat, stations), f32),
                pltpu.VMEM((flat, stations), f32),
                pltpu.VMEM((stations, 2 * stations), f32),
                pltpu.VMEM((clusters, 8, stations), f32),
                pltpu.VMEM((pair, stations), f32),
                pltpu.VMEM((pair, stations), f32),
                pltpu.VMEM((n_chan, 8, small), f32),
                pltpu.VMEM((n_chan, 8, small), f32),
                pltpu.VMEM((pair, lanes), f32),
                pltpu.VMEM((n_dir, pair, lanes), f32),
                pltpu.VMEM((pair, lanes), f32),
                pltpu.VMEM((n_chan, pair, lanes), f32),
                dma((n_dir,)),
                dma((n_dir,)),
                dma((n_dir,)),
                dma((n_dir,)),
                dma((n_chan,)),
                dma((n_chan,)),
                dma((n_chan,)),
                dma((n_chan,)),
                dma((n_dir,)),
                dma((n_dir,)),
                dma((n_chan,)),
                dma((n_chan,)),
            ],
            compiler_params=pltpu.CompilerParams(collective_id=0, has_side_effects=True),
            name="calibrate",
        )(
            visibilities[0],
            station_uv,
            table,
            band_offset,
            gains_init,
            duals_init,
            poly,
            penalty.reshape(1, clusters),
            harmonics,
            threshold,
        )
        return gains, duals, consensus.reshape(2, clusters, stations * NTERM)

    return jax.shard_map(
        shards,
        mesh=mesh,
        in_specs=(
            P("chan", None, None, None),
            P(),
            P(None, "dir", None),
            P("dir", None),
            P("chan"),
            P(None, "dir", "chan", None),
            P(None, "dir", "chan", None),
            P(None, "dir", None),
            P("dir"),
            P(),
            P(),
        ),
        out_specs=(
            P(None, "dir", "chan", None),
            P(None, "dir", "chan", None),
            P(None, "dir", None),
        ),
        check_vma=False,
    )
```

```python
import functools
import math

import jax
import jax.numpy as jnp
import numpy as np
from jax import lax
from jax.experimental import pallas as pl
from jax.experimental.pallas import tpu as pltpu
from jax.sharding import PartitionSpec as P

NTERM = 4
SWEEPS = 2
MESH = pl.DeviceIdType.MESH
highest = lax.Precision.HIGHEST
VM = pl.BlockSpec(memory_space=pltpu.VMEM)


def fit_circle():
    nodes = np.cos(np.pi * (np.arange(400) + 0.5) / 800.0) * 0.5
    square = nodes * nodes
    scale = 0.25
    sine = np.polynomial.chebyshev.Chebyshev.fit(
        square, np.sin(2 * np.pi * nodes) / nodes, 5, domain=[0, scale], w=nodes
    ).convert(kind=np.polynomial.Polynomial)
    cosine = np.polynomial.chebyshev.Chebyshev.fit(
        square, np.cos(2 * np.pi * nodes), 6, domain=[0, scale]
    ).convert(kind=np.polynomial.Polynomial)
    return [float(c) for c in sine.coef], [float(c) for c in cosine.coef]


SINE, COSINE = fit_circle()


def horner(coefs, x):
    total = coefs[-1] * x + coefs[-2]
    for c in coefs[-3::-1]:
        total = total * x + c
    return total


def circle(turns):
    r = turns - jnp.round(turns)
    square = r * r
    return horner(COSINE, square), r * horner(SINE, square)


def legendre(x):
    return [
        jnp.ones_like(x),
        x,
        0.5 * (3.0 * x * x - 1.0),
        0.5 * (5.0 * x * x * x - 3.0 * x),
    ]


def split(x):
    high = x.astype(jnp.bfloat16)
    low = (x - high.astype(jnp.float32)).astype(jnp.bfloat16)
    return high, low


def tdot(a, b):
    return lax.dot_general(a, b, (((0,), (0,)), ((), ())), preferred_element_type=jnp.float32)


def meet(n_dir, n_chan, me_d, me_c):
    barrier = pltpu.get_barrier_semaphore()
    for j in range(1, n_dir):
        pl.semaphore_signal(
            barrier, inc=1, device_id={"dir": lax.rem(me_d + j, n_dir)}, device_id_type=MESH
        )
    for j in range(1, n_chan):
        pl.semaphore_signal(
            barrier, inc=1, device_id={"chan": lax.rem(me_c + j, n_chan)}, device_id_type=MESH
        )
    pl.semaphore_wait(barrier, n_dir + n_chan - 2)


def column(pen):
    count = pen.shape[1]
    row = lax.broadcasted_iota(jnp.int32, (count, count), 0)
    col = lax.broadcasted_iota(jnp.int32, (count, count), 1)
    return jnp.sum(jnp.where(row == col, pen[...], 0.0), axis=1, keepdims=True)


def step_kernel(
    n_dir,
    n_chan,
    sources,
    vis,
    uv,
    table,
    band,
    g_ref,
    dual_ref,
    poly,
    pen_ref,
    harm,
    cut,
    gains_out,
    dual_out,
    cons_out,
    b_ref,
    g_all,
    s_all,
    b_all,
    src_t,
    er,
    ei,
    macc,
    rows,
    dual,
    gains,
    packed,
    zin,
    own,
    zall,
    part,
    blocks,
    gs,
    gr,
    ss,
    sr,
    bs,
    br,
    s1,
    r1,
    s2,
    r2,
    s3,
    r3,
):
    pair, stations = dual.shape
    clusters = pair // 2
    me_d, me_c = lax.axis_index("dir"), lax.axis_index("chan")
    b_ref[...] = jnp.full(b_ref.shape, band[0], jnp.float32)

    def send(src, dst, a, b, peer):
        return pltpu.make_async_remote_copy(
            src_ref=src, dst_ref=dst, send_sem=a, recv_sem=b, device_id=peer, device_id_type=MESH
        )

    meet(n_dir, n_chan, me_d, me_c)
    copies = []
    for j in range(1, n_dir):
        peer = {"dir": lax.rem(me_d + n_dir - j, n_dir)}
        copies.append(send(g_ref, g_all.at[j], gs.at[j], gr.at[j], peer))
        copies.append(send(table, s_all.at[j], ss.at[j], sr.at[j], peer))
    for j in range(1, n_chan):
        peer = {"chan": lax.rem(me_c + n_chan - j, n_chan)}
        copies.append(send(b_ref, b_all.at[j], bs.at[j], br.at[j], peer))
    for c in copies:
        c.start()
    b_all[0] = b_ref[...]
    g_all[0] = g_ref[...]

    here = b_ref[0:1, 0:1]
    stretch = 1.0 + 0.25 * here
    u = uv[0:1, :] * stretch
    v = uv[1:2, :] * stretch
    chunk = math.gcd(clusters, 4)
    chunks = clusters // chunk
    span = chunk * sources
    macc[:, :stations] = jnp.zeros((stations, stations), jnp.float32)

    def step(d, c, keep):
        start = pl.multiple_of(c * span, span)
        cols = src_t[pl.ds(start, span), :]
        weight = cols[:, 2:3]
        e_r, e_i = circle(cols[:, 0:1] * u + cols[:, 1:2] * v)
        if keep:
            er[pl.ds(start, span), :] = e_r
            ei[pl.ds(start, span), :] = e_i
        f_r, f_i = [], []
        for i in range(chunk):
            a = g_all[d, 0, c * chunk + i]
            b = g_all[d, 1, c * chunk + i]
            part_r = e_r[i * sources : (i + 1) * sources]
            part_i = e_i[i * sources : (i + 1) * sources]
            f_r.append(part_r * a - part_i * b)
            f_i.append(part_r * b + part_i * a)
        f_r = jnp.concatenate(f_r, axis=0)
        f_i = jnp.concatenate(f_i, axis=0)
        lh, ll = split(jnp.concatenate([f_r * weight, f_i * weight], axis=0))
        high, low = split(jnp.concatenate([f_r - f_i, f_i + f_r], axis=0))
        macc[:, :stations] += tdot(lh, high) + (tdot(lh, low) + tdot(ll, high))

    src_t[...] = jnp.transpose(table[...])
    lax.fori_loop(0, chunks, lambda c, x: (step(0, c, True), x)[1], 0)

    for k in range(clusters):
        dual[k : k + 1, :] = dual_ref[0, k]
        dual[clusters + k : clusters + k + 1, :] = dual_ref[1, k]
    level = legendre(here)
    pen = column(pen_ref)
    pull = jnp.concatenate([pen, pen], axis=0)
    tile = 32 * NTERM
    tiles = stations // 32
    row = lax.broadcasted_iota(jnp.int32, (tile, tile), 0)
    col = lax.broadcasted_iota(jnp.int32, (tile, tile), 1)
    pick = jnp.zeros((tile, tile), jnp.float32)
    for t in range(NTERM):
        pick = jnp.where(row - NTERM * col == t, level[t], pick)
    stacked = jnp.concatenate([poly[:, j * tile : (j + 1) * tile] for j in range(tiles)], axis=0)
    value = jnp.dot(stacked, pick, precision=highest)
    value = jnp.concatenate(
        [value[j * pair : (j + 1) * pair, :32] for j in range(tiles)], axis=1
    )
    offset = dual[...] / pull
    goal = (value - offset) * pull
    for k in range(clusters):
        rows[k, 0:1, :] = g_ref[0, k]
        rows[k, 1:2, :] = g_ref[1, k]
        rows[k, 2:3, :] = goal[k : k + 1]
        rows[k, 3:4, :] = goal[clusters + k : clusters + k + 1]
        rows[k, 4:5, :] = jnp.broadcast_to(pen[k : k + 1, :], (1, stations))
        rows[k, 5:8, :] = jnp.zeros((3, stations), jnp.float32)

    for c in copies:
        c.wait()

    def others(d, carry):
        src_t[...] = jnp.transpose(s_all[d])
        lax.fori_loop(0, chunks, lambda c, x: (step(d, c, False), x)[1], 0)
        return carry

    lax.fori_loop(1, n_dir, others, 0)
    src_t[...] = jnp.transpose(table[...])
    both = macc[:, :stations]
    turned = jnp.transpose(both)
    macc[:, :stations] = vis[:, 0, :] - 0.5 * (both + turned)
    macc[:, stations:] = vis[:, 1, :] - 0.5 * (both - turned)

    def solve(k, carry):
        start = pl.multiple_of(k * sources, sources)
        e_r = er[pl.ds(start, sources), :]
        e_i = ei[pl.ds(start, sources), :]
        weight = src_t[pl.ds(start, sources), :][:, 2:3]
        left = jnp.concatenate([e_r * weight, e_i * weight], axis=0)
        near = left.astype(jnp.bfloat16).astype(jnp.float32)
        turned_left = jnp.transpose(jnp.concatenate([near, left - near], axis=0))
        turned_left = turned_left.astype(jnp.bfloat16)
        rh, rl = split(
            jnp.concatenate(
                [jnp.concatenate([e_r, e_i], axis=0), jnp.concatenate([-e_i, e_r], axis=0)],
                axis=1,
            )
        )
        coherency = jnp.dot(
            jnp.concatenate([turned_left, turned_left], axis=1),
            jnp.concatenate([rh, rh, rl, rl], axis=0),
            preferred_element_type=jnp.float32,
        )
        c_r = coherency[:, :stations]
        c_i = coherency[:, stations:]
        r_r = macc[:, :stations]
        r_i = macc[:, stations:]
        power = c_r * c_r + c_i * c_i
        b_r = r_r * c_r + r_i * c_i
        b_i = r_i * c_r - r_r * c_i
        block = rows[k]
        g_r, g_i = block[0:1], block[1:2]
        rho = block[4:5]
        g_2 = g_r * g_r + g_i * g_i
        cols = jnp.transpose(jnp.concatenate([block[0:2], g_2, block[3:8]], axis=0))
        k_r, k_i = cols[:, 0:1], cols[:, 1:2]
        n_r = jnp.sum(b_r * k_r + b_i * k_i, axis=0, keepdims=True)
        n_i = jnp.sum(b_r * k_i - b_i * k_r, axis=0, keepdims=True)
        total = jnp.sum(power * cols[:, 2:3], axis=0, keepdims=True)
        inverse = 1.0 / (total + rho)
        h_r = (n_r + g_r * total + block[2:3]) * inverse
        h_i = (n_i + g_i * total + block[3:4]) * inverse
        mix_r = g_r * h_r + g_i * h_i
        mix_i = g_r * h_i - g_i * h_r
        h_2 = h_r * h_r + h_i * h_i
        cols = jnp.transpose(jnp.concatenate([h_r, h_i, mix_r, mix_i, h_2, block[5:8]], axis=0))
        q_r, q_i = cols[:, 0:1], cols[:, 1:2]
        m_r = jnp.sum(b_r * q_r + b_i * q_i, axis=0, keepdims=True)
        m_i = jnp.sum(b_r * q_i - b_i * q_r, axis=0, keepdims=True)
        t_0 = jnp.sum(power * cols[:, 2:3], axis=0, keepdims=True)
        t_1 = jnp.sum(power * cols[:, 3:4], axis=0, keepdims=True)
        t_2 = jnp.sum(power * cols[:, 4:5], axis=0, keepdims=True)
        inverse = 1.0 / (t_2 + block[4:5])
        new_r = (m_r + g_r * t_0 - g_i * t_1 + block[2:3]) * inverse
        new_i = (m_i + g_r * t_1 + g_i * t_0 + block[3:4]) * inverse
        gains[pl.ds(k, 1), :] = new_r
        gains[pl.ds(clusters + k, 1), :] = new_i
        gains_out[0, k] = new_r
        gains_out[1, k] = new_i
        return carry

    lax.fori_loop(0, clusters, solve, 0)

    spread = gains[...] + offset
    each = stations // n_chan
    groups = pair // 8
    used = groups * each
    lanes = packed.shape[2]
    for j in range(n_chan):
        if used < lanes:
            packed[j] = jnp.zeros((8, lanes), jnp.float32)
        packed[j, :, :used] = jnp.concatenate(
            [spread[8 * g : 8 * g + 8, j * each : (j + 1) * each] for g in range(groups)], axis=1
        )

    first = []
    for j in range(1, n_chan):
        peer = lax.rem(me_c + n_chan - j, n_chan)
        first.append(send(packed.at[peer], zin.at[j], s1.at[j], r1.at[j], {"chan": peer}))
    for c in first:
        c.start()

    everywhere = b_all[:, 0, :]
    values = legendre(everywhere)
    gram = [
        [jnp.sum(values[t] * values[s], axis=0, keepdims=True) for s in range(t + 1)]
        for t in range(NTERM)
    ]
    factor = [[None] * NTERM for _ in range(NTERM)]
    for t in range(NTERM):
        for s in range(t + 1):
            rest_sum = gram[t][s]
            for r in range(s):
                rest_sum = rest_sum - factor[t][r] * factor[s][r]
            factor[t][s] = jnp.sqrt(rest_sum) if s == t else rest_sum / factor[s][s]
    half = []
    for t in range(NTERM):
        rest_sum = values[t]
        for s in range(t):
            rest_sum = rest_sum - factor[t][s] * half[s]
        half.append(rest_sum / factor[t][t])
    taps = [None] * NTERM
    for t in reversed(range(NTERM)):
        rest_sum = half[t]
        for s in range(t + 1, NTERM):
            rest_sum = rest_sum - factor[s][t] * taps[s]
        taps[t] = rest_sum / factor[t][t]

    mixed = [packed[me_c] * taps[t][0:1, 0:1] for t in range(NTERM)]
    for j in range(1, n_chan):
        first[j - 1].wait_recv()
        got = zin[j]
        for t in range(NTERM):
            mixed[t] = mixed[t] + got * taps[t][j : j + 1, 0:1]
    wide = NTERM * each
    if wide < own.shape[1]:
        own[...] = jnp.zeros_like(own)
    for g in range(groups):
        own[8 * g : 8 * g + 8, :wide] = jnp.concatenate(
            [mixed[t][:, g * each : (g + 1) * each] for t in range(NTERM)], axis=1
        )
    second = []
    for j in range(1, n_dir):
        peer = lax.rem(me_d + j, n_dir)
        second.append(send(own, zall.at[me_d], s2.at[j], r2.at[j], {"dir": peer}))
    for c in second:
        c.start()
    zall[me_d] = own[...]
    for c in second:
        c.wait()
    width = own.shape[1]
    coeff_r = jnp.concatenate([zall[d][:clusters] for d in range(n_dir)], axis=0)
    coeff_i = jnp.concatenate([zall[d][clusters:] for d in range(n_dir)], axis=0)
    a = lax.dot_general(
        harm[...],
        jnp.concatenate([coeff_r, coeff_i], axis=1),
        (((0,), (0,)), ((), ())),
        precision=highest,
        preferred_element_type=jnp.float32,
    )
    a_r, a_i = a[:, :width], a[:, width:]
    size = jnp.sqrt(a_r * a_r + a_i * a_i)
    limit = cut[0]
    scale = jnp.maximum(size - limit, 0.0) / jnp.maximum(size, limit)
    mine = harm[pl.ds(pl.multiple_of(me_d * clusters, clusters), clusters), :]
    done = jnp.dot(
        mine, jnp.concatenate([a_r * scale, a_i * scale], axis=1), precision=highest
    )
    part[:clusters] = done[:, :width]
    part[clusters:] = done[:, width:]
    third = []
    for j in range(1, n_chan):
        peer = lax.rem(me_c + j, n_chan)
        third.append(send(part, blocks.at[me_c], s3.at[j], r3.at[j], {"chan": peer}))
    for c in third:
        c.start()
    blocks[me_c] = part[...]
    row = lax.broadcasted_iota(jnp.int32, (width, width), 0)
    col = lax.broadcasted_iota(jnp.int32, (width, width), 1)
    weave = jnp.zeros((width, width), jnp.float32)
    sample = jnp.zeros((width, width), jnp.float32)
    for t in range(NTERM):
        place = row - t * each
        inside = (place >= 0) & (place < each)
        weave = jnp.where(inside & (col == NTERM * place + t), 1.0, weave)
        sample = jnp.where(inside & (col == place), level[t], sample)
    for c in first:
        c.wait_send()
    for c in third:
        c.wait()
    result = jnp.dot(
        jnp.concatenate([blocks[j] for j in range(n_chan)], axis=0),
        jnp.concatenate([weave, sample], axis=1),
        precision=highest,
    )
    fitted = []
    for j in range(n_chan):
        piece = result[j * pair : (j + 1) * pair]
        cons_out[:, j * wide : (j + 1) * wide] = piece[:, :wide]
        fitted.append(piece[:, width : width + each])
    fitted = jnp.concatenate(fitted, axis=1)
    fresh = dual[...] + pull * (gains[...] - fitted)
    for k in range(clusters):
        dual_out[0, k] = fresh[k : k + 1]
        dual_out[1, k] = fresh[clusters + k : clusters + k + 1]


def solution(mesh):
    n_dir, n_chan = mesh.shape["dir"], mesh.shape["chan"]

    def shards(
        visibilities,
        station_uv,
        source_lm,
        source_flux,
        band_offset,
        gains_init,
        duals_init,
        poly_init,
        penalty,
        harmonics,
        threshold,
    ):
        f32 = jnp.float32
        _, clusters, sources = source_lm.shape
        stations = station_uv.shape[1]
        pair = 2 * clusters
        lanes = max(128, stations * NTERM // n_chan)
        poly = poly_init.reshape(pair, stations * NTERM)
        flat = clusters * sources
        table = jnp.concatenate(
            [
                source_lm.reshape(2, flat),
                source_flux.reshape(1, flat),
                jnp.zeros((5, flat), f32),
            ],
            axis=0,
        )
        dma = pltpu.SemaphoreType.DMA
        shape = (2, clusters, 1, stations)
        small = max(128, stations // n_chan * (pair // 8))
        SM = pl.BlockSpec(memory_space=pltpu.SMEM)
        gains, duals, consensus = pl.pallas_call(
            functools.partial(step_kernel, n_dir, n_chan, sources),
            out_shape=(
                jax.ShapeDtypeStruct(shape, f32),
                jax.ShapeDtypeStruct(shape, f32),
                jax.ShapeDtypeStruct((pair, stations * NTERM), f32),
            ),
            in_specs=[VM, VM, VM, SM, VM, VM, VM, VM, VM, SM],
            out_specs=(VM,) * 3,
            scratch_shapes=[
                pltpu.VMEM((8, 128), f32),
                pltpu.VMEM((n_dir,) + shape, f32),
                pltpu.VMEM((n_dir, 8, flat), f32),
                pltpu.VMEM((n_chan, 8, 128), f32),
                pltpu.VMEM((flat, 8), f32),
                pltpu.VMEM((flat, stations), f32),
                pltpu.VMEM((flat, stations), f32),
                pltpu.VMEM((stations, 2 * stations), f32),
                pltpu.VMEM((clusters, 8, stations), f32),
                pltpu.VMEM((pair, stations), f32),
                pltpu.VMEM((pair, stations), f32),
                pltpu.VMEM((n_chan, 8, small), f32),
                pltpu.VMEM((n_chan, 8, small), f32),
                pltpu.VMEM((pair, lanes), f32),
                pltpu.VMEM((n_dir, pair, lanes), f32),
                pltpu.VMEM((pair, lanes), f32),
                pltpu.VMEM((n_chan, pair, lanes), f32),
                dma((n_dir,)),
                dma((n_dir,)),
                dma((n_dir,)),
                dma((n_dir,)),
                dma((n_chan,)),
                dma((n_chan,)),
                dma((n_chan,)),
                dma((n_chan,)),
                dma((n_dir,)),
                dma((n_dir,)),
                dma((n_chan,)),
                dma((n_chan,)),
            ],
            compiler_params=pltpu.CompilerParams(collective_id=0, has_side_effects=True),
            name="calibrate",
        )(
            visibilities[0],
            station_uv,
            table,
            band_offset,
            gains_init,
            duals_init,
            poly,
            penalty.reshape(1, clusters),
            harmonics,
            threshold,
        )
        return gains, duals, consensus.reshape(2, clusters, stations * NTERM)

    return jax.shard_map(
        shards,
        mesh=mesh,
        in_specs=(
            P("chan", None, None, None),
            P(),
            P(None, "dir", None),
            P("dir", None),
            P("chan"),
            P(None, "dir", "chan", None),
            P(None, "dir", "chan", None),
            P(None, "dir", None),
            P("dir"),
            P(),
            P(),
        ),
        out_specs=(
            P(None, "dir", "chan", None),
            P(None, "dir", "chan", None),
            P(None, "dir", None),
        ),
        check_vma=False,
    )
```

```python
import functools
import math

import jax
import jax.numpy as jnp
import numpy as np
from jax import lax
from jax.experimental import pallas as pl
from jax.experimental.pallas import tpu as pltpu
from jax.sharding import PartitionSpec as P

NTERM = 4
SWEEPS = 2
MESH = pl.DeviceIdType.MESH
highest = lax.Precision.HIGHEST
VM = pl.BlockSpec(memory_space=pltpu.VMEM)


def fit_circle():
    nodes = np.cos(np.pi * (np.arange(400) + 0.5) / 800.0) * 0.5
    square = nodes * nodes
    scale = 0.25
    sine = np.polynomial.chebyshev.Chebyshev.fit(
        square, np.sin(2 * np.pi * nodes) / nodes, 5, domain=[0, scale], w=nodes
    ).convert(kind=np.polynomial.Polynomial)
    cosine = np.polynomial.chebyshev.Chebyshev.fit(
        square, np.cos(2 * np.pi * nodes), 6, domain=[0, scale]
    ).convert(kind=np.polynomial.Polynomial)
    return [float(c) for c in sine.coef], [float(c) for c in cosine.coef]


SINE, COSINE = fit_circle()


def horner(coefs, x):
    total = coefs[-1] * x + coefs[-2]
    for c in coefs[-3::-1]:
        total = total * x + c
    return total


def circle(turns):
    r = turns - jnp.round(turns)
    square = r * r
    return horner(COSINE, square), r * horner(SINE, square)


def legendre(x):
    return [
        jnp.ones_like(x),
        x,
        0.5 * (3.0 * x * x - 1.0),
        0.5 * (5.0 * x * x * x - 3.0 * x),
    ]


def split(x):
    high = x.astype(jnp.bfloat16)
    low = (x - high.astype(jnp.float32)).astype(jnp.bfloat16)
    return high, low


def tdot(a, b):
    return lax.dot_general(a, b, (((0,), (0,)), ((), ())), preferred_element_type=jnp.float32)


def meet(n_dir, n_chan, me_d, me_c):
    barrier = pltpu.get_barrier_semaphore()
    for j in range(1, n_dir):
        pl.semaphore_signal(
            barrier, inc=1, device_id={"dir": lax.rem(me_d + j, n_dir)}, device_id_type=MESH
        )
    for j in range(1, n_chan):
        pl.semaphore_signal(
            barrier, inc=1, device_id={"chan": lax.rem(me_c + j, n_chan)}, device_id_type=MESH
        )
    pl.semaphore_wait(barrier, n_dir + n_chan - 2)


def column(pen):
    count = pen.shape[1]
    row = lax.broadcasted_iota(jnp.int32, (count, count), 0)
    col = lax.broadcasted_iota(jnp.int32, (count, count), 1)
    return jnp.sum(jnp.where(row == col, pen[...], 0.0), axis=1, keepdims=True)


def step_kernel(
    n_dir,
    n_chan,
    sources,
    vis,
    uv,
    table,
    band,
    g_ref,
    dual_ref,
    poly,
    pen_ref,
    harm,
    cut,
    gains_out,
    dual_out,
    cons_out,
    b_ref,
    g_all,
    s_all,
    b_all,
    src_t,
    er,
    ei,
    macc,
    rows,
    dual,
    gains,
    packed,
    zin,
    own,
    zall,
    part,
    blocks,
    gs,
    gr,
    ss,
    sr,
    bs,
    br,
    s1,
    r1,
    s2,
    r2,
    s3,
    r3,
):
    pair, stations = dual.shape
    clusters = pair // 2
    me_d, me_c = lax.axis_index("dir"), lax.axis_index("chan")
    b_ref[...] = jnp.full(b_ref.shape, band[0], jnp.float32)

    def send(src, dst, a, b, peer):
        return pltpu.make_async_remote_copy(
            src_ref=src, dst_ref=dst, send_sem=a, recv_sem=b, device_id=peer, device_id_type=MESH
        )

    meet(n_dir, n_chan, me_d, me_c)
    copies = []
    for j in range(1, n_dir):
        peer = {"dir": lax.rem(me_d + n_dir - j, n_dir)}
        copies.append(send(g_ref, g_all.at[j], gs.at[j], gr.at[j], peer))
        copies.append(send(table, s_all.at[j], ss.at[j], sr.at[j], peer))
    for j in range(1, n_chan):
        peer = {"chan": lax.rem(me_c + n_chan - j, n_chan)}
        copies.append(send(b_ref, b_all.at[j], bs.at[j], br.at[j], peer))
    for c in copies:
        c.start()
    b_all[0] = b_ref[...]
    g_all[0] = g_ref[...]

    here = b_ref[0:1, 0:1]
    stretch = 1.0 + 0.25 * here
    u = uv[0:1, :] * stretch
    v = uv[1:2, :] * stretch
    chunk = math.gcd(clusters, 4)
    chunks = clusters // chunk
    span = chunk * sources
    macc[:, :stations] = jnp.zeros((stations, stations), jnp.float32)

    def step(d, c, keep):
        start = pl.multiple_of(c * span, span)
        cols = src_t[pl.ds(start, span), :]
        weight = cols[:, 2:3]
        e_r, e_i = circle(cols[:, 0:1] * u + cols[:, 1:2] * v)
        if keep:
            er[pl.ds(start, span), :] = e_r
            ei[pl.ds(start, span), :] = e_i
        f_r, f_i = [], []
        for i in range(chunk):
            a = g_all[d, 0, c * chunk + i]
            b = g_all[d, 1, c * chunk + i]
            part_r = e_r[i * sources : (i + 1) * sources]
            part_i = e_i[i * sources : (i + 1) * sources]
            f_r.append(part_r * a - part_i * b)
            f_i.append(part_r * b + part_i * a)
        f_r = jnp.concatenate(f_r, axis=0)
        f_i = jnp.concatenate(f_i, axis=0)
        lh, ll = split(jnp.concatenate([f_r * weight, f_i * weight], axis=0))
        high, low = split(jnp.concatenate([f_r - f_i, f_i + f_r], axis=0))
        macc[:, :stations] += tdot(lh, high) + (tdot(lh, low) + tdot(ll, high))

    src_t[...] = jnp.transpose(table[...])
    lax.fori_loop(0, chunks, lambda c, x: (step(0, c, True), x)[1], 0)

    for k in range(clusters):
        dual[k : k + 1, :] = dual_ref[0, k]
        dual[clusters + k : clusters + k + 1, :] = dual_ref[1, k]
    level = legendre(here)
    pen = column(pen_ref)
    pull = jnp.concatenate([pen, pen], axis=0)
    tile = 32 * NTERM
    tiles = stations // 32
    row = lax.broadcasted_iota(jnp.int32, (tile, tile), 0)
    col = lax.broadcasted_iota(jnp.int32, (tile, tile), 1)
    pick = jnp.zeros((tile, tile), jnp.float32)
    for t in range(NTERM):
        pick = jnp.where(row - NTERM * col == t, level[t], pick)
    stacked = jnp.concatenate([poly[:, j * tile : (j + 1) * tile] for j in range(tiles)], axis=0)
    value = jnp.dot(stacked, pick, precision=highest)
    value = jnp.concatenate(
        [value[j * pair : (j + 1) * pair, :32] for j in range(tiles)], axis=1
    )
    offset = dual[...] / pull
    goal = (value - offset) * pull
    for k in range(clusters):
        rows[k, 0:1, :] = g_ref[0, k]
        rows[k, 1:2, :] = g_ref[1, k]
        rows[k, 2:3, :] = goal[k : k + 1]
        rows[k, 3:4, :] = goal[clusters + k : clusters + k + 1]
        rows[k, 4:5, :] = jnp.broadcast_to(pen[k : k + 1, :], (1, stations))
        rows[k, 5:8, :] = jnp.zeros((3, stations), jnp.float32)

    for c in copies:
        c.wait()

    def others(d, carry):
        src_t[...] = jnp.transpose(s_all[d])
        lax.fori_loop(0, chunks, lambda c, x: (step(d, c, False), x)[1], 0)
        return carry

    lax.fori_loop(1, n_dir, others, 0)
    src_t[...] = jnp.transpose(table[...])
    both = macc[:, :stations]
    turned = jnp.transpose(both)
    macc[:, :stations] = vis[:, 0, :] - 0.5 * (both + turned)
    macc[:, stations:] = vis[:, 1, :] - 0.5 * (both - turned)

    def solve(k, carry):
        start = pl.multiple_of(k * sources, sources)
        e_r = er[pl.ds(start, sources), :]
        e_i = ei[pl.ds(start, sources), :]
        weight = src_t[pl.ds(start, sources), :][:, 2:3]
        left = jnp.concatenate([e_r * weight, e_i * weight], axis=0)
        near = left.astype(jnp.bfloat16).astype(jnp.float32)
        turned_left = jnp.transpose(jnp.concatenate([near, left - near], axis=0))
        turned_left = turned_left.astype(jnp.bfloat16)
        rh, rl = split(
            jnp.concatenate(
                [jnp.concatenate([e_r, e_i], axis=0), jnp.concatenate([-e_i, e_r], axis=0)],
                axis=1,
            )
        )
        coherency = jnp.dot(
            jnp.concatenate([turned_left, turned_left], axis=1),
            jnp.concatenate([rh, rh, rl, rl], axis=0),
            preferred_element_type=jnp.float32,
        )
        c_r = coherency[:, :stations]
        c_i = coherency[:, stations:]
        r_r = macc[:, :stations]
        r_i = macc[:, stations:]
        power = c_r * c_r + c_i * c_i
        b_r = r_r * c_r + r_i * c_i
        b_i = r_i * c_r - r_r * c_i
        block = rows[k]
        g_r, g_i = block[0:1], block[1:2]
        rho = block[4:5]
        g_2 = g_r * g_r + g_i * g_i
        cols = jnp.transpose(jnp.concatenate([block[0:2], g_2, block[3:8]], axis=0))
        k_r, k_i = cols[:, 0:1], cols[:, 1:2]
        n_r = jnp.sum(b_r * k_r + b_i * k_i, axis=0, keepdims=True)
        n_i = jnp.sum(b_r * k_i - b_i * k_r, axis=0, keepdims=True)
        total = jnp.sum(power * cols[:, 2:3], axis=0, keepdims=True)
        inverse = 1.0 / (total + rho)
        h_r = (n_r + g_r * total + block[2:3]) * inverse
        h_i = (n_i + g_i * total + block[3:4]) * inverse
        mix_r = g_r * h_r + g_i * h_i
        mix_i = g_r * h_i - g_i * h_r
        h_2 = h_r * h_r + h_i * h_i
        cols = jnp.transpose(jnp.concatenate([h_r, h_i, mix_r, mix_i, h_2, block[5:8]], axis=0))
        q_r, q_i = cols[:, 0:1], cols[:, 1:2]
        m_r = jnp.sum(b_r * q_r + b_i * q_i, axis=0, keepdims=True)
        m_i = jnp.sum(b_r * q_i - b_i * q_r, axis=0, keepdims=True)
        t_0 = jnp.sum(power * cols[:, 2:3], axis=0, keepdims=True)
        t_1 = jnp.sum(power * cols[:, 3:4], axis=0, keepdims=True)
        t_2 = jnp.sum(power * cols[:, 4:5], axis=0, keepdims=True)
        inverse = 1.0 / (t_2 + block[4:5])
        new_r = (m_r + g_r * t_0 - g_i * t_1 + block[2:3]) * inverse
        new_i = (m_i + g_r * t_1 + g_i * t_0 + block[3:4]) * inverse
        gains[pl.ds(k, 1), :] = new_r
        gains[pl.ds(clusters + k, 1), :] = new_i
        gains_out[0, k] = new_r
        gains_out[1, k] = new_i
        return carry

    batch = math.gcd(clusters, 2)

    def solve_batch(b, carry):
        for i in range(batch):
            solve(b * batch + i, carry)
        return carry

    lax.fori_loop(0, clusters // batch, solve_batch, 0)

    spread = gains[...] + offset
    each = stations // n_chan
    groups = pair // 8
    used = groups * each
    lanes = packed.shape[2]
    for j in range(n_chan):
        if used < lanes:
            packed[j] = jnp.zeros((8, lanes), jnp.float32)
        packed[j, :, :used] = jnp.concatenate(
            [spread[8 * g : 8 * g + 8, j * each : (j + 1) * each] for g in range(groups)], axis=1
        )

    first = []
    for j in range(1, n_chan):
        peer = lax.rem(me_c + n_chan - j, n_chan)
        first.append(send(packed.at[peer], zin.at[j], s1.at[j], r1.at[j], {"chan": peer}))
    for c in first:
        c.start()

    everywhere = b_all[:, 0, :]
    values = legendre(everywhere)
    gram = [
        [jnp.sum(values[t] * values[s], axis=0, keepdims=True) for s in range(t + 1)]
        for t in range(NTERM)
    ]
    factor = [[None] * NTERM for _ in range(NTERM)]
    for t in range(NTERM):
        for s in range(t + 1):
            rest_sum = gram[t][s]
            for r in range(s):
                rest_sum = rest_sum - factor[t][r] * factor[s][r]
            factor[t][s] = jnp.sqrt(rest_sum) if s == t else rest_sum / factor[s][s]
    half = []
    for t in range(NTERM):
        rest_sum = values[t]
        for s in range(t):
            rest_sum = rest_sum - factor[t][s] * half[s]
        half.append(rest_sum / factor[t][t])
    taps = [None] * NTERM
    for t in reversed(range(NTERM)):
        rest_sum = half[t]
        for s in range(t + 1, NTERM):
            rest_sum = rest_sum - factor[s][t] * taps[s]
        taps[t] = rest_sum / factor[t][t]

    mixed = [packed[me_c] * taps[t][0:1, 0:1] for t in range(NTERM)]
    for j in range(1, n_chan):
        first[j - 1].wait_recv()
        got = zin[j]
        for t in range(NTERM):
            mixed[t] = mixed[t] + got * taps[t][j : j + 1, 0:1]
    wide = NTERM * each
    if wide < own.shape[1]:
        own[...] = jnp.zeros_like(own)
    for g in range(groups):
        own[8 * g : 8 * g + 8, :wide] = jnp.concatenate(
            [mixed[t][:, g * each : (g + 1) * each] for t in range(NTERM)], axis=1
        )
    second = []
    for j in range(1, n_dir):
        peer = lax.rem(me_d + j, n_dir)
        second.append(send(own, zall.at[me_d], s2.at[j], r2.at[j], {"dir": peer}))
    for c in second:
        c.start()
    zall[me_d] = own[...]
    for c in second:
        c.wait()
    width = own.shape[1]
    coeff_r = jnp.concatenate([zall[d][:clusters] for d in range(n_dir)], axis=0)
    coeff_i = jnp.concatenate([zall[d][clusters:] for d in range(n_dir)], axis=0)
    a = lax.dot_general(
        harm[...],
        jnp.concatenate([coeff_r, coeff_i], axis=1),
        (((0,), (0,)), ((), ())),
        precision=highest,
        preferred_element_type=jnp.float32,
    )
    a_r, a_i = a[:, :width], a[:, width:]
    size = jnp.sqrt(a_r * a_r + a_i * a_i)
    limit = cut[0]
    scale = jnp.maximum(size - limit, 0.0) / jnp.maximum(size, limit)
    mine = harm[pl.ds(pl.multiple_of(me_d * clusters, clusters), clusters), :]
    done = jnp.dot(
        mine, jnp.concatenate([a_r * scale, a_i * scale], axis=1), precision=highest
    )
    part[:clusters] = done[:, :width]
    part[clusters:] = done[:, width:]
    third = []
    for j in range(1, n_chan):
        peer = lax.rem(me_c + j, n_chan)
        third.append(send(part, blocks.at[me_c], s3.at[j], r3.at[j], {"chan": peer}))
    for c in third:
        c.start()
    blocks[me_c] = part[...]
    row = lax.broadcasted_iota(jnp.int32, (width, width), 0)
    col = lax.broadcasted_iota(jnp.int32, (width, width), 1)
    weave = jnp.zeros((width, width), jnp.float32)
    sample = jnp.zeros((width, width), jnp.float32)
    for t in range(NTERM):
        place = row - t * each
        inside = (place >= 0) & (place < each)
        weave = jnp.where(inside & (col == NTERM * place + t), 1.0, weave)
        sample = jnp.where(inside & (col == place), level[t], sample)
    for c in first:
        c.wait_send()
    for c in third:
        c.wait()
    result = jnp.dot(
        jnp.concatenate([blocks[j] for j in range(n_chan)], axis=0),
        jnp.concatenate([weave, sample], axis=1),
        precision=highest,
    )
    fitted = []
    for j in range(n_chan):
        piece = result[j * pair : (j + 1) * pair]
        cons_out[:, j * wide : (j + 1) * wide] = piece[:, :wide]
        fitted.append(piece[:, width : width + each])
    fitted = jnp.concatenate(fitted, axis=1)
    fresh = dual[...] + pull * (gains[...] - fitted)
    for k in range(clusters):
        dual_out[0, k] = fresh[k : k + 1]
        dual_out[1, k] = fresh[clusters + k : clusters + k + 1]


def emit_kernel(a, b, c, a_out, b_out, c_out):
    a_out[...] = a[...]
    b_out[...] = b[...]
    c_out[...] = c[...]


def solution(mesh):
    n_dir, n_chan = mesh.shape["dir"], mesh.shape["chan"]

    def shards(
        visibilities,
        station_uv,
        source_lm,
        source_flux,
        band_offset,
        gains_init,
        duals_init,
        poly_init,
        penalty,
        harmonics,
        threshold,
    ):
        f32 = jnp.float32
        _, clusters, sources = source_lm.shape
        stations = station_uv.shape[1]
        pair = 2 * clusters
        lanes = max(128, stations * NTERM // n_chan)
        poly = poly_init.reshape(pair, stations * NTERM)
        flat = clusters * sources
        table = jnp.concatenate(
            [
                source_lm.reshape(2, flat),
                source_flux.reshape(1, flat),
                jnp.zeros((5, flat), f32),
            ],
            axis=0,
        )
        dma = pltpu.SemaphoreType.DMA
        shape = (2, clusters, 1, stations)
        small = max(128, stations // n_chan * (pair // 8))
        SM = pl.BlockSpec(memory_space=pltpu.SMEM)
        gains, duals, consensus = pl.pallas_call(
            functools.partial(step_kernel, n_dir, n_chan, sources),
            out_shape=(
                jax.ShapeDtypeStruct(shape, f32),
                jax.ShapeDtypeStruct(shape, f32),
                jax.ShapeDtypeStruct((pair, stations * NTERM), f32),
            ),
            in_specs=[VM, VM, VM, SM, VM, VM, VM, VM, VM, SM],
            out_specs=(VM,) * 3,
            scratch_shapes=[
                pltpu.VMEM((8, 128), f32),
                pltpu.VMEM((n_dir,) + shape, f32),
                pltpu.VMEM((n_dir, 8, flat), f32),
                pltpu.VMEM((n_chan, 8, 128), f32),
                pltpu.VMEM((flat, 8), f32),
                pltpu.VMEM((flat, stations), f32),
                pltpu.VMEM((flat, stations), f32),
                pltpu.VMEM((stations, 2 * stations), f32),
                pltpu.VMEM((clusters, 8, stations), f32),
                pltpu.VMEM((pair, stations), f32),
                pltpu.VMEM((pair, stations), f32),
                pltpu.VMEM((n_chan, 8, small), f32),
                pltpu.VMEM((n_chan, 8, small), f32),
                pltpu.VMEM((pair, lanes), f32),
                pltpu.VMEM((n_dir, pair, lanes), f32),
                pltpu.VMEM((pair, lanes), f32),
                pltpu.VMEM((n_chan, pair, lanes), f32),
                dma((n_dir,)),
                dma((n_dir,)),
                dma((n_dir,)),
                dma((n_dir,)),
                dma((n_chan,)),
                dma((n_chan,)),
                dma((n_chan,)),
                dma((n_chan,)),
                dma((n_dir,)),
                dma((n_dir,)),
                dma((n_chan,)),
                dma((n_chan,)),
            ],
            compiler_params=pltpu.CompilerParams(collective_id=0, has_side_effects=True),
            name="calibrate",
        )(
            visibilities[0],
            station_uv,
            table,
            band_offset,
            gains_init,
            duals_init,
            poly,
            penalty.reshape(1, clusters),
            harmonics,
            threshold,
        )
        gains, duals, consensus = pl.pallas_call(
            emit_kernel,
            out_shape=(
                jax.ShapeDtypeStruct(shape, f32),
                jax.ShapeDtypeStruct(shape, f32),
                jax.ShapeDtypeStruct((pair, stations * NTERM), f32),
            ),
            in_specs=[VM] * 3,
            out_specs=(VM,) * 3,
            name="emit",
        )(gains, duals, consensus)
        return gains, duals, consensus.reshape(2, clusters, stations * NTERM)

    return jax.shard_map(
        shards,
        mesh=mesh,
        in_specs=(
            P("chan", None, None, None),
            P(),
            P(None, "dir", None),
            P("dir", None),
            P("chan"),
            P(None, "dir", "chan", None),
            P(None, "dir", "chan", None),
            P(None, "dir", None),
            P("dir"),
            P(),
            P(),
        ),
        out_specs=(
            P(None, "dir", "chan", None),
            P(None, "dir", "chan", None),
            P(None, "dir", None),
        ),
        check_vma=False,
    )
```
